32 devices in a mesh: gx: 4 (over y, core), gy: 2 (over x), ch: 4 (over z).
Axes of the slice: x: 2, y: 2, z: 4, core: 2. Of those that a mesh axis runs over, the one named last changes fastest.
Arguments:
- density: bfloat16 [4, 32, 128, 128], P('gx', 'gy', 'ch'), may hold values from -6 to 6
- first_kernel: bfloat16 [3, 3, 3, 128, 128], P(None, None, None, 'ch'), may hold values from -0.109375 to 0.109375
- first_bias: float32 [128], P('ch'), may hold values from -3 to 3
- second_kernel: bfloat16 [3, 3, 3, 128, 128], P(None, None, None, 'ch'), may hold values from -0.109375 to 0.109375
- second_bias: float32 [128], P('ch'), may hold values from -3 to 3
Outputs:
- features: bfloat16 [4, 32, 128, 128], P('gx', 'gy', 'ch')
The draws below stay inside these ranges and needn't reach their ends.
All inputs are finite; a program needn't handle non-finite values.
Results may differ from the reference program's by a relative error of at most 0.0045.
Values may be sent and summed in bfloat16 or wider, within the bound.
No kernel may reach another device: no remote copies, remote signals or barrier semaphores. Data moves between devices by JAX's collectives and lax.ppermute only.
A program may use at most 64 MiB of HBM per device.

```python
import jax
import jax.numpy as jnp
from jax import lax

C = 128
NZ = 128
NX = 4
NY = 32


def steps_of(rng, extent, shards, low, largest):
    level, own = 1.0, jax.random.fold_in(rng, 6)
    for dim, shards_of in shards:
        steps = jnp.exp(jax.random.uniform(jax.random.fold_in(own, dim), (shards_of,), jnp.float32, low / len(shards), largest / len(shards)))
        level = level * jnp.repeat(steps, extent[dim] // shards_of).reshape([-1 if axis == dim else 1 for axis in range(len(extent))])
    return level


def scatter_about(stream_key, dims, scale, limit, shards=(), kind=jnp.bfloat16):
    values = jax.random.normal(stream_key, dims, jnp.float32) * scale
    if len(shards) > 0:
        values = steps_of(stream_key, dims, shards, -0.22, 0.18) * values
    return jnp.clip(values, min=-limit, max=limit).astype(kind)


def setup_inputs(seed: int = 0) -> dict:
    streams_of = jax.random.split(jax.random.key(seed), 6)
    density = scatter_about(streams_of[0], (NX, NY, C, NZ), 1.0, 6.0, ((0, 4), (1, 2), (2, 4)))
    first_kernel = scatter_about(streams_of[1], (3, 3, 3, C, C), (27 * C) ** -0.5, 0.109375, ((3, 4),))
    first_bias = scatter_about(streams_of[2], (C,), 0.5, 3.0, ((0, 4),), jnp.float32)
    second_kernel = scatter_about(streams_of[3], (3, 3, 3, C, C), (27 * C) ** -0.5, 0.109375, ((3, 4),))
    second_bias = scatter_about(streams_of[4], (C,), 0.5, 3.0, ((0, 4),), jnp.float32)
    return {"density": density, "first_kernel": first_kernel, "first_bias": first_bias, "second_kernel": second_kernel, "second_bias": second_bias}


def convolve(field, kernel, bias):
    volume = field.astype(jnp.float32).transpose(2, 0, 1, 3)[None]
    weights = kernel.astype(jnp.float32).transpose(3, 4, 0, 1, 2)
    result = lax.conv_general_dilated(volume, weights, (1, 1, 1), ((1, 1), (1, 1), (1, 1)), dimension_numbers=("NCDHW", "OIDHW", "NCDHW"), precision=lax.Precision.HIGHEST)
    result = result[0].transpose(1, 2, 0, 3) + bias.reshape(1, 1, -1, 1)
    return jnp.maximum(result, 0.0).astype(jnp.bfloat16)


def reference(density, first_kernel, first_bias, second_kernel, second_bias):
    hidden = convolve(density, first_kernel, first_bias)
    return convolve(hidden, second_kernel, second_bias)
```

```python
import functools

import jax
import jax.numpy as jnp
from jax import lax
from jax.experimental import pallas as pl
from jax.experimental.pallas import tpu as pltpu
from jax.sharding import PartitionSpec as P


def shifted(block, axis, step):
    count = lax.axis_size(axis)
    pairs = [(i, i + step) for i in range(count) if 0 <= i + step < count]
    return lax.ppermute(block, axis, pairs)


def gathered(block, axis):
    count = lax.axis_size(axis)
    return [block] + [
        lax.ppermute(block, axis, [(i, (i + step) % count) for i in range(count)])
        for step in range(1, count)
    ]


def taps_kernel(count, place_ref, kernel_ref, *refs):
    blocks, (below_ref, center_ref, above_ref, volume, weights) = refs[:count], refs[count:]
    rows, outputs, depth = center_ref.shape
    part = blocks[0].shape[1]
    inputs = part * count
    place = place_ref[0]
    for step, block in enumerate(blocks):
        source = lax.rem(place - step + count, count)
        volume[:, pl.ds(pl.multiple_of(source * part, part), part), :] = block[...]
    for a in range(3):
        for b in range(3):
            for c in range(3):
                first = (a * 3 + c) * outputs
                weights[first : first + outputs, b * inputs : (b + 1) * inputs] = kernel_ref[a, b, c]
    lane = lax.broadcasted_iota(jnp.int32, (outputs, depth), 1)
    taps = weights[...]
    for y in range(0, rows, 2):
        window = jnp.concatenate(
            [volume[y + i : y + i + 3].reshape(3 * inputs, depth) for i in range(2)], axis=1
        )
        product = jnp.dot(taps, window, preferred_element_type=jnp.float32)
        for i in range(2):
            for a, out in enumerate((above_ref, center_ref, below_ref)):
                first, middle, last = (
                    product[(a * 3 + c) * outputs : (a * 3 + c + 1) * outputs, i * depth : (i + 1) * depth]
                    for c in range(3)
                )
                total = (
                    middle
                    + jnp.where(lane == 0, 0.0, pltpu.roll(first, 1, 1))
                    + jnp.where(lane == depth - 1, 0.0, pltpu.roll(last, depth - 1, 1))
                )
                out[y + i] = total.astype(out.dtype)


def plane_terms(blocks, kernel):
    count = len(blocks)
    rows, part, depth = blocks[0].shape
    rows, outputs = rows - 2, kernel.shape[3]
    place = lax.axis_index("ch").astype(jnp.int32).reshape(1)
    vmem = pl.BlockSpec(memory_space=pltpu.VMEM)
    return pl.pallas_call(
        functools.partial(taps_kernel, count),
        out_shape=[
            jax.ShapeDtypeStruct((rows, outputs, depth), dtype)
            for dtype in (jnp.bfloat16, jnp.float32, jnp.bfloat16)
        ],
        in_specs=[pl.BlockSpec(memory_space=pltpu.SMEM)] + [vmem] * (count + 1),
        out_specs=[vmem] * 3,
        scratch_shapes=[
            pltpu.VMEM((rows + 2, part * count, depth), jnp.bfloat16),
            pltpu.VMEM((9 * outputs, 3 * part * count), jnp.bfloat16),
        ],
        name="taps",
    )(place, kernel, *blocks)


def layer(field, kernel, bias):
    before = shifted(field[-1:], "gy", 1)
    after = shifted(field[:1], "gy", -1)
    padded = jnp.concatenate([before, field, after], axis=0)
    below, center, above = plane_terms(gathered(padded, "ch"), kernel)
    total = center + shifted(above, "gx", 1).astype(jnp.float32) + shifted(below, "gx", -1).astype(jnp.float32)
    return jnp.maximum(total + bias.reshape(1, -1, 1), 0.0).astype(jnp.bfloat16)


def per_device(density, first_kernel, first_bias, second_kernel, second_bias):
    hidden = layer(density[0], first_kernel, first_bias)
    return layer(hidden, second_kernel, second_bias)[None]


def solution(mesh):
    placed = (
        P("gx", "gy", "ch", None),
        P(None, None, None, "ch", None),
        P("ch"),
        P(None, None, None, "ch", None),
        P("ch"),
    )
    return jax.shard_map(
        per_device, mesh=mesh, in_specs=placed, out_specs=P("gx", "gy", "ch", None), check_vma=False
    )
```

```python
import functools

import jax
import jax.numpy as jnp
from jax import lax
from jax.experimental import pallas as pl
from jax.experimental.pallas import tpu as pltpu
from jax.sharding import PartitionSpec as P

VMEM_BYTES = 12 << 20


def on_chip(array):
    return pltpu.with_memory_space_constraint(array, pltpu.VMEM)


def call(kernel, name, out_shape, scratch, *operands):
    vmem = pl.BlockSpec(memory_space=pltpu.VMEM)
    return pl.pallas_call(
        kernel,
        out_shape=out_shape,
        in_specs=[vmem] * len(operands),
        out_specs=jax.tree.map(lambda _: vmem, out_shape),
        scratch_shapes=scratch,
        compiler_params=pltpu.CompilerParams(vmem_limit_bytes=VMEM_BYTES),
        name=name,
    )(*operands)


def partners(count):
    return [[(i, i ^ step) for i in range(count)] for step in range(count)]


def channel_swaps(block):
    steps = partners(lax.axis_size("ch"))
    return [block] + [lax.ppermute(block, "ch", pairs) for pairs in steps[1:]]


def edge_moves(edge, rows_step):
    rows, channels = lax.axis_size("gy"), lax.axis_size("ch")
    moved = []
    for pairs in partners(channels):
        if rows == 2:
            along = [(0, 1), (1, 0)]
        else:
            along = [(i, i + rows_step) for i in range(rows) if 0 <= i + rows_step < rows]
        both = [(i * channels + c, j * channels + d) for i, j in along for c, d in pairs]
        moved.append(lax.ppermute(edge, ("gy", "ch"), both))
    return moved


def taps_kernel(count, kernel_ref, *refs):
    blocks, refs = refs[:count], refs[count:]
    edges, (near_ref, center_ref, far_ref, volume, weights) = refs[:-5], refs[-5:]
    befores, afters = edges[:count], edges[-count:]
    rows, outputs, depth = center_ref.shape
    part = blocks[0].shape[1]
    inputs = part * count
    place = lax.axis_index("ch")
    gy, gx = lax.axis_index("gy"), lax.axis_index("gx")
    has_before = jnp.full((1, part, depth), gy > 0)
    has_after = jnp.full((1, part, depth), gy < lax.axis_size("gy") - 1)
    for step in range(count):
        source = jnp.bitwise_xor(place, step)
        here = pl.ds(pl.multiple_of(source * part, part), part)
        volume[1 : rows + 1, here, :] = blocks[step][...]
        volume[0:1, here, :] = jnp.where(has_before, befores[step][...], 0.0)
        volume[rows + 1 : rows + 2, here, :] = jnp.where(has_after, afters[step][...], 0.0)
    even = gx % 2 == 0
    near = jnp.where(even, 0, 2)
    outer = jnp.full((outputs, inputs), (gx == 0) | (gx == lax.axis_size("gx") - 1))
    for slot, a in enumerate((near, 1, 2 - near)):
        for b in range(3):
            for c in range(3):
                first = (slot * 3 + c) * outputs
                tap = kernel_ref[a, b, c]
                if slot == 2:
                    tap = jnp.where(outer, 0.0, tap)
                weights[first : first + outputs, b * inputs : (b + 1) * inputs] = tap
    lane = lax.broadcasted_iota(jnp.int32, (outputs, depth), 1)
    taps = weights[...]
    for y in range(0, rows, 2):
        window = jnp.concatenate(
            [volume[y + i : y + i + 3].reshape(3 * inputs, depth) for i in range(2)], axis=1
        )
        product = jnp.dot(taps, window, preferred_element_type=jnp.float32)
        for i in range(2):
            for slot, out in enumerate((near_ref, center_ref, far_ref)):
                first, middle, last = (
                    product[(slot * 3 + c) * outputs : (slot * 3 + c + 1) * outputs, i * depth : (i + 1) * depth]
                    for c in range(3)
                )
                total = (
                    middle
                    + jnp.where(lane == 0, 0.0, pltpu.roll(first, 1, 1))
                    + jnp.where(lane == depth - 1, 0.0, pltpu.roll(last, depth - 1, 1))
                )
                out[y + i] = total.astype(out.dtype)


def finish_kernel(near_ref, center_ref, far_ref, bias_ref, out_ref, *edge_refs):
    total = center_ref[...] + near_ref[...].astype(jnp.float32) + far_ref[...].astype(jnp.float32)
    out_ref[...] = jnp.maximum(total + bias_ref[...][None], 0.0).astype(out_ref.dtype)
    rows = out_ref.shape[0]
    if len(edge_refs) == 1:
        edge_refs[0][0] = out_ref[jnp.where(lax.axis_index("gy") == 0, rows - 1, 0)]
    if len(edge_refs) == 2:
        edge_refs[0][0] = out_ref[rows - 1]
        edge_refs[1][0] = out_ref[0]


def layer(field, edges, kernel, bias, last):
    rows, part, depth = field.shape
    outputs = kernel.shape[3]
    count = lax.axis_size("ch")
    blocks = channel_swaps(field)
    halos = [moved for edge, step in zip(edges, (1, -1)) for moved in edge_moves(edge, step)]
    near, center, far = call(
        functools.partial(taps_kernel, count),
        "taps",
        [pltpu.VMEM((rows, outputs, depth), dtype) for dtype in (jnp.bfloat16, jnp.float32, jnp.bfloat16)],
        [
            pltpu.VMEM((rows + 2, part * count, depth), jnp.bfloat16),
            pltpu.VMEM((9 * outputs, 3 * part * count), jnp.bfloat16),
        ],
        on_chip(kernel),
        *[on_chip(block) for block in blocks],
        *[on_chip(halo) for halo in halos],
    )
    planes = lax.axis_size("gx")
    near = lax.ppermute(near, "gx", [(i, i ^ 1) for i in range(planes)])
    outer = [(0, 0), (planes - 1, planes - 1)]
    inner = [(i, i + 1) for i in range(1, planes - 1, 2)]
    far = lax.ppermute(far, "gx", outer + inner + [(j, i) for i, j in inner])
    if last:
        out_shape = [jax.ShapeDtypeStruct((rows, outputs, depth), jnp.bfloat16)]
    else:
        out_shape = [pltpu.VMEM((rows, outputs, depth), jnp.bfloat16)]
        out_shape += [pltpu.VMEM((1, outputs, depth), jnp.bfloat16)] * len(edges)
    return call(
        finish_kernel, "finish", out_shape, [], on_chip(near), on_chip(center), on_chip(far), on_chip(bias)
    )


def per_device(density, first_kernel, first_bias, second_kernel, second_bias):
    density = density[0]
    if lax.axis_size("gy") == 2:
        row = jnp.where(lax.axis_index("gy") == 0, density.shape[0] - 1, 0)
        edges = [lax.dynamic_slice_in_dim(density, row, 1, 0)]
    else:
        edges = [density[-1:], density[:1]]
    first_bias, second_bias = first_bias.reshape(-1, 1), second_bias.reshape(-1, 1)
    hidden, *edges = layer(density, edges, first_kernel, first_bias, False)
    return layer(hidden, edges, second_kernel, second_bias, True)[0][None]


def solution(mesh):
    placed = (
        P("gx", "gy", "ch", None),
        P(None, None, None, "ch", None),
        P("ch"),
        P(None, None, None, "ch", None),
        P("ch"),
    )
    return jax.shard_map(
        per_device, mesh=mesh, in_specs=placed, out_specs=P("gx", "gy", "ch", None), check_vma=False
    )
```

```python
import functools

import jax
import jax.numpy as jnp
from jax import lax
from jax.experimental import pallas as pl
from jax.experimental.pallas import tpu as pltpu
from jax.sharding import PartitionSpec as P

VMEM_BYTES = 12 << 20
VMEM = pltpu.VMEM


def call(kernel, name, out_shape, *operands, stored=(), scratch=(), flops=0):
    spec = pl.BlockSpec(memory_space=VMEM)
    return pl.pallas_call(
        kernel,
        out_shape=out_shape,
        in_specs=[pl.BlockSpec(memory_space=pltpu.HBM)] * len(stored) + [spec] * len(operands),
        out_specs=[spec] * len(out_shape),
        scratch_shapes=scratch,
        compiler_params=pltpu.CompilerParams(vmem_limit_bytes=VMEM_BYTES),
        cost_estimate=pl.CostEstimate(flops=flops, bytes_accessed=0, transcendentals=0),
        name=name,
    )(
        *[pltpu.with_memory_space_constraint(operand, pltpu.HBM) for operand in stored],
        *[pltpu.with_memory_space_constraint(operand, VMEM) for operand in operands],
    )


def sides():
    return 1 if lax.axis_size("gy") == 2 else 2


def partners():
    count = lax.axis_size("ch")
    return [[(i, i ^ step) for i in range(count)] for step in range(count)]


def channel_swaps(block):
    return [lax.ppermute(block, "ch", pairs) for pairs in partners()[1:]]


def edge_moves(edge, step, pairings):
    rows, channels = lax.axis_size("gy"), lax.axis_size("ch")
    if rows == 2:
        along = [(0, 1), (1, 0)]
    else:
        along = [(i, i + step) for i in range(rows) if 0 <= i + step < rows]
    return [
        lax.ppermute(edge, ("gy", "ch"), [(i * channels + c, j * channels + d) for i, j in along for c, d in pairs])
        for pairs in pairings
    ]


def prepare_kernel(*refs):
    stored, (_, first_taps, second_taps, first_bias, second_bias, own), refs = refs[:5], refs[5:11], refs[11:]
    copies, first_ref, second_ref, *bias_refs = refs
    moves = [
        pltpu.make_async_copy(source, target, copies.at[i])
        for i, (source, target) in enumerate(zip(stored, (first_ref, second_ref, *bias_refs, own)))
    ]
    for move in moves:
        move.start()
    for move in moves:
        move.wait()
    gx = lax.axis_index("gx")
    outputs, inputs = first_ref.shape[3:]
    far = jnp.where(gx % 2 == 0, 2, 0)
    outer = jnp.full((outputs, inputs), (gx == 0) | (gx == lax.axis_size("gx") - 1))
    for kernel_ref, out in ((first_ref, first_taps), (second_ref, second_taps)):
        for slot, a in enumerate((far, 2 - far, 1)):
            for b in range(3):
                for c in range(3):
                    tap = kernel_ref[a, b, c]
                    if slot == 0:
                        tap = jnp.where(outer, 0.0, tap)
                    first = (slot * 3 + c) * outputs
                    out[first : first + outputs, b * inputs : (b + 1) * inputs] = tap
    at = [lax.broadcasted_iota(jnp.int32, (outputs, outputs), axis) for axis in range(2)]
    for bias_ref, out in zip(bias_refs, (first_bias, second_bias)):
        column = jnp.sum(jnp.where(at[0] == at[1], bias_ref[...], 0.0), axis=1, keepdims=True)
        out[...] = jnp.broadcast_to(column, out.shape)


def terms(taps, volume, slots, outs):
    rows, outputs, depth = outs[0].shape
    inputs = volume.shape[1]
    lane = lax.broadcasted_iota(jnp.int32, (outputs, depth), 1)
    for y in [*range(0, rows - 1, 2)] + [rows - 2] * (rows % 2):
        window = jnp.concatenate(
            [volume[y + i : y + i + 3].reshape(3 * inputs, depth) for i in range(2)], axis=1
        )
        product = jnp.dot(taps, window, preferred_element_type=jnp.float32)
        for i in range(2):
            for slot, out in zip(slots, outs):
                first, middle, last = (
                    product[(slot * 3 + c) * outputs : (slot * 3 + c + 1) * outputs, i * depth : (i + 1) * depth]
                    for c in range(3)
                )
                total = (
                    middle
                    + jnp.where(lane == 0, 0.0, pltpu.roll(first, 1, 1))
                    + jnp.where(lane == depth - 1, 0.0, pltpu.roll(last, depth - 1, 1))
                )
                out[y + i] = total.astype(out.dtype)


def beside_kernel(count, halo, taps_ref, *refs):
    (far_ref, near_ref, volume), refs = refs[-3:], refs[:-3]
    blocks, halos = refs[:count], refs[count:]
    rows, part, depth = blocks[0].shape
    place, low = lax.axis_index("ch"), lax.axis_index("gy") == 0
    if sides() == 1:
        own, beside = jnp.where(low, 1, halo), jnp.where(low, 1 + rows, 0)
        outside = jnp.where(low, 0, volume.shape[0] - 1)
        volume[outside] = jnp.zeros((part * count, depth), volume.dtype)
    else:
        own = halo
    def channels(step):
        source = jnp.bitwise_xor(place, step % count)
        return pl.ds(pl.multiple_of(source * part, part), part)

    for step in range(count):
        volume[pl.ds(own, rows), channels(step), :] = blocks[step][...]
    step = 0
    for ref in halos:
        for first in range(0, ref.shape[0], halo):
            if sides() == 1:
                at = beside
            else:
                at = 0 if step < count else halo + rows
            volume[pl.ds(at, halo), channels(step), :] = ref[first : first + halo]
            step += 1
    span = 3 * far_ref.shape[1]
    terms(taps_ref[: 2 * span], volume, (0, 1), (far_ref, near_ref))


def center_kernel(taps_ref, volume, center_ref):
    terms(taps_ref[6 * center_ref.shape[1] :], volume, (0,), (center_ref,))


def finish_kernel(near_ref, center_ref, far_ref, bias_ref, out_ref):
    total = center_ref[...] + near_ref[...].astype(jnp.float32) + far_ref[...].astype(jnp.float32)
    out_ref[...] = jnp.maximum(total + bias_ref[...][None], 0.0).astype(out_ref.dtype)


def hidden_kernel(near_ref, center_ref, far_ref, bias_ref, out_ref):
    finish_kernel(near_ref, center_ref, far_ref, bias_ref, out_ref)
    if lax.axis_size("gy") > 2:
        gy, rows = lax.axis_index("gy"), out_ref.shape[0]
        for row, outside in ((0, gy == 0), (rows - 1, gy == lax.axis_size("gy") - 1)):
            kept = out_ref[row]
            out_ref[row] = jnp.where(jnp.full(kept.shape, outside), 0.0, kept)


def layer(blocks, halos, halo, rows, taps, bias, kernel, out_type):
    count = len(blocks)
    _, part, depth = blocks[0].shape
    outputs = taps.shape[0] // 9
    flops = 2 * rows * depth * taps.shape[0] * taps.shape[1]
    side = VMEM((rows, outputs, depth), jnp.bfloat16)
    far, near, volume = call(
        functools.partial(beside_kernel, count, halo),
        "beside",
        [side, side, VMEM((rows + 2, part * count, depth), jnp.bfloat16)],
        taps,
        *blocks,
        *halos,
        flops=2 * flops // 3,
    )
    planes = lax.axis_size("gx")
    inner = [(i, i + 1) for i in range(1, planes - 1, 2)]
    outer = [(0, 0), (planes - 1, planes - 1)]
    far = lax.ppermute(far, "gx", outer + inner + [(j, i) for i, j in inner])
    near = lax.ppermute(near, "gx", [(i, i ^ 1) for i in range(planes)])
    (center,) = call(
        center_kernel, "center", [VMEM((rows, outputs, depth), jnp.float32)], taps, volume, flops=flops // 3
    )
    (out,) = call(
        kernel,
        "finish",
        [out_type((rows, outputs, depth), jnp.bfloat16)],
        near,
        center,
        far,
        bias,
    )
    return out


def per_device(density, first_kernel, first_bias, second_kernel, second_bias):
    density = density[0]
    rows, part, depth = density.shape
    outputs = first_kernel.shape[3]
    count = lax.axis_size("ch")
    pairings = partners()
    if sides() == 1:
        start = jnp.where(lax.axis_index("gy") == 0, rows - 2, 0)
        halos = edge_moves(lax.dynamic_slice_in_dim(density, start, 2, 0), 1, pairings[:2])
        last = lax.ppermute(density, "ch", pairings[-1])
        nearest = lax.ppermute(density, "ch", pairings[1])
    else:
        halos = edge_moves(density[-2:], 1, pairings) + edge_moves(density[:2], -1, pairings)
        others = channel_swaps(density)
    taps_shape = VMEM((9 * outputs, 3 * part * count), jnp.bfloat16)
    bias_shape = VMEM((outputs, depth), jnp.float32)
    first_taps, second_taps, first_bias, second_bias, own = call(
        prepare_kernel,
        "prepare",
        [taps_shape, taps_shape, bias_shape, bias_shape, VMEM(density.shape, density.dtype)],
        halos[0],
        stored=(first_kernel, second_kernel, first_bias.reshape(1, -1), second_bias.reshape(1, -1), density),
        scratch=[
            pltpu.SemaphoreType.DMA((5,)),
            *[VMEM(kernel.shape, kernel.dtype) for kernel in (first_kernel, second_kernel)],
            *[VMEM((1, outputs), jnp.float32)] * 2,
        ],
    )
    if sides() == 1:
        place = lax.axis_index("ch")
        inner = (place == 1) | (place == 2)
        handed = lax.ppermute(jnp.where(inner, last, own), "ch", [(0, 2), (3, 1), (1, 0), (2, 3)])
        others = [nearest, handed, last]
        pair, _ = lax.optimization_barrier((jnp.concatenate(halos, axis=0), last))
        halos = [pair, lax.ppermute(pair, "ch", pairings[2])]
    hidden = layer(
        [own, *others], halos, 2, rows + sides(), first_taps, first_bias, hidden_kernel, VMEM
    )
    blocks = [hidden, *channel_swaps(hidden)]
    out = layer(blocks, [], 0, rows, second_taps, second_bias, finish_kernel, jax.ShapeDtypeStruct)
    return out[None]


def solution(mesh):
    placed = (
        P("gx", "gy", "ch", None),
        P(None, None, None, "ch", None),
        P("ch"),
        P(None, None, None, "ch", None),
        P("ch"),
    )
    return jax.shard_map(
        per_device, mesh=mesh, in_specs=placed, out_specs=P("gx", "gy", "ch", None), check_vma=False
    )
```

```python
import functools

import jax
import jax.numpy as jnp
from jax import lax
from jax.experimental import pallas as pl
from jax.experimental.pallas import tpu as pltpu
from jax.sharding import PartitionSpec as P

VMEM_BYTES = 12 << 20
VMEM = pltpu.VMEM


def call(kernel, name, out_shape, *operands, stored=(), scratch=(), flops=0):
    spec = pl.BlockSpec(memory_space=VMEM)
    return pl.pallas_call(
        kernel,
        out_shape=out_shape,
        in_specs=[pl.BlockSpec(memory_space=pltpu.HBM)] * len(stored) + [spec] * len(operands),
        out_specs=[spec] * len(out_shape),
        scratch_shapes=scratch,
        compiler_params=pltpu.CompilerParams(vmem_limit_bytes=VMEM_BYTES),
        cost_estimate=pl.CostEstimate(flops=flops, bytes_accessed=0, transcendentals=0),
        name=name,
    )(
        *[pltpu.with_memory_space_constraint(operand, pltpu.HBM) for operand in stored],
        *[pltpu.with_memory_space_constraint(operand, VMEM) for operand in operands],
    )


def sides():
    return 1 if lax.axis_size("gy") == 2 else 2


def partners():
    count = lax.axis_size("ch")
    return [[(i, i ^ step) for i in range(count)] for step in range(count)]


def channel_swaps(block):
    return [lax.ppermute(block, "ch", pairs) for pairs in partners()[1:]]


def edge_moves(edge, step, pairings):
    rows, channels = lax.axis_size("gy"), lax.axis_size("ch")
    if rows == 2:
        along = [(0, 1), (1, 0)]
    else:
        along = [(i, i + step) for i in range(rows) if 0 <= i + step < rows]
    return [
        lax.ppermute(edge, ("gy", "ch"), [(i * channels + c, j * channels + d) for i, j in along for c, d in pairs])
        for pairs in pairings
    ]


def far_pairs(idle):
    planes, rows = lax.axis_size("gx"), lax.axis_size("gy")
    pairs = [(i, i + 1, g, g) for i in range(1, planes - 1, 2) for g in range(rows)]
    if idle:
        alone = [(i * rows + g, i * rows + g) for i in (0, planes - 1) for g in range(rows)]
    else:
        alone = []
        pairs += [(i, i, g, g + 1) for i in (0, planes - 1) for g in range(0, rows, 2)]
    there = [(i * rows + g, j * rows + h) for i, j, g, h in pairs]
    return alone + there + [(j, i) for i, j in there]


def prepare_kernel(*refs):
    stored, (_, first_taps, second_taps, first_bias, second_bias, own), refs = refs[:5], refs[5:11], refs[11:]
    copies, first_ref, second_ref, *bias_refs = refs
    moves = [
        pltpu.make_async_copy(source, target, copies.at[i])
        for i, (source, target) in enumerate(zip(stored, (first_ref, second_ref, *bias_refs, own)))
    ]
    for move in moves:
        move.start()
    for move in moves:
        move.wait()
    gx = lax.axis_index("gx")
    outputs, inputs = first_ref.shape[3:]
    far = jnp.where(gx % 2 == 0, 2, 0)
    outer = jnp.full((outputs, inputs), (gx == 0) | (gx == lax.axis_size("gx") - 1))
    for kernel_ref, out in ((first_ref, first_taps), (second_ref, second_taps)):
        for slot, a in enumerate((far, 2 - far, 1)):
            for b in range(3):
                for c in range(3):
                    tap = kernel_ref[a, b, c]
                    if slot == 0:
                        tap = jnp.where(outer, 0.0, tap)
                    first = (slot * 3 + c) * outputs
                    out[first : first + outputs, b * inputs : (b + 1) * inputs] = tap
    at = [lax.broadcasted_iota(jnp.int32, (outputs, outputs), axis) for axis in range(2)]
    for bias_ref, out in zip(bias_refs, (first_bias, second_bias)):
        column = jnp.sum(jnp.where(at[0] == at[1], bias_ref[...], 0.0), axis=1, keepdims=True)
        out[...] = jnp.broadcast_to(column, out.shape)


def terms(taps, volume, slots, outs):
    rows, outputs, depth = outs[0].shape
    inputs = volume.shape[1]
    lane = lax.broadcasted_iota(jnp.int32, (outputs, depth), 1)
    for y in [*range(0, rows - 1, 2)] + [rows - 2] * (rows % 2):
        window = jnp.concatenate(
            [volume[y + i : y + i + 3].reshape(3 * inputs, depth) for i in range(2)], axis=1
        )
        product = jnp.dot(taps, window, preferred_element_type=jnp.float32)
        for i in range(2):
            for slot, out in zip(slots, outs):
                first, middle, last = (
                    product[(slot * 3 + c) * outputs : (slot * 3 + c + 1) * outputs, i * depth : (i + 1) * depth]
                    for c in range(3)
                )
                total = (
                    middle
                    + jnp.where(lane == 0, 0.0, pltpu.roll(first, 1, 1))
                    + jnp.where(lane == depth - 1, 0.0, pltpu.roll(last, depth - 1, 1))
                )
                out[y + i] = total.astype(out.dtype)


def beside_kernel(count, halo, taps_ref, *refs):
    (far_ref, near_ref, volume), refs = refs[-3:], refs[:-3]
    blocks, halos = refs[:count], refs[count:]
    rows, part, depth = blocks[0].shape
    place, low = lax.axis_index("ch"), lax.axis_index("gy") == 0
    if sides() == 1:
        own, beside = jnp.where(low, 1, halo), jnp.where(low, 1 + rows, 0)
        outside = jnp.where(low, 0, volume.shape[0] - 1)
        volume[outside] = jnp.zeros((part * count, depth), volume.dtype)
    else:
        own = halo
    def channels(step):
        source = jnp.bitwise_xor(place, step % count)
        return pl.ds(pl.multiple_of(source * part, part), part)

    for step in range(count):
        volume[pl.ds(own, rows), channels(step), :] = blocks[step][...]
    step = 0
    for ref in halos:
        for first in range(0, ref.shape[0], halo):
            if sides() == 1:
                at = beside
            else:
                at = 0 if step < count else halo + rows
            volume[pl.ds(at, halo), channels(step), :] = ref[first : first + halo]
            step += 1
    span = 3 * far_ref.shape[1]
    terms(taps_ref[: 2 * span], volume, (0, 1), (far_ref, near_ref))


def center_kernel(taps_ref, volume, center_ref):
    terms(taps_ref[6 * center_ref.shape[1] :], volume, (0,), (center_ref,))


def finish_kernel(near_ref, center_ref, far_ref, bias_ref, out_ref):
    total = center_ref[...] + near_ref[...].astype(jnp.float32) + far_ref[...].astype(jnp.float32)
    out_ref[...] = jnp.maximum(total + bias_ref[...][None], 0.0).astype(out_ref.dtype)


def hidden_kernel(near_ref, center_ref, far_ref, bias_ref, out_ref):
    finish_kernel(near_ref, center_ref, far_ref, bias_ref, out_ref)
    if lax.axis_size("gy") > 2:
        gy, rows = lax.axis_index("gy"), out_ref.shape[0]
        for row, outside in ((0, gy == 0), (rows - 1, gy == lax.axis_size("gy") - 1)):
            kept = out_ref[row]
            out_ref[row] = jnp.where(jnp.full(kept.shape, outside), 0.0, kept)


def layer(blocks, halos, halo, rows, taps, bias, kernel, out_type, idle):
    count = len(blocks)
    _, part, depth = blocks[0].shape
    outputs = taps.shape[0] // 9
    flops = 2 * rows * depth * taps.shape[0] * taps.shape[1]
    side = VMEM((rows, outputs, depth), jnp.bfloat16)
    far, near, volume = call(
        functools.partial(beside_kernel, count, halo),
        "beside",
        [side, side, VMEM((rows + 2, part * count, depth), jnp.bfloat16)],
        taps,
        *blocks,
        *halos,
        flops=2 * flops // 3,
    )
    planes = lax.axis_size("gx")
    far = lax.ppermute(far, ("gx", "gy"), far_pairs(idle))
    near = lax.ppermute(near, "gx", [(i, i ^ 1) for i in range(planes)])
    (center,) = call(
        center_kernel, "center", [VMEM((rows, outputs, depth), jnp.float32)], taps, volume, flops=flops // 3
    )
    (out,) = call(
        kernel,
        "finish",
        [out_type((rows, outputs, depth), jnp.bfloat16)],
        near,
        center,
        far,
        bias,
    )
    return out


def per_device(density, first_kernel, first_bias, second_kernel, second_bias):
    density = density[0]
    rows, part, depth = density.shape
    outputs = first_kernel.shape[3]
    count = lax.axis_size("ch")
    pairings = partners()
    if sides() == 1:
        start = jnp.where(lax.axis_index("gy") == 0, rows - 2, 0)
        halos = edge_moves(lax.dynamic_slice_in_dim(density, start, 2, 0), 1, pairings[:2])
        last = lax.ppermute(density, "ch", pairings[-1])
        nearest = lax.ppermute(density, "ch", pairings[1])
    else:
        halos = edge_moves(density[-2:], 1, pairings) + edge_moves(density[:2], -1, pairings)
        others = channel_swaps(density)
    taps_shape = VMEM((9 * outputs, 3 * part * count), jnp.bfloat16)
    bias_shape = VMEM((outputs, depth), jnp.float32)
    first_taps, second_taps, first_bias, second_bias, own = call(
        prepare_kernel,
        "prepare",
        [taps_shape, taps_shape, bias_shape, bias_shape, VMEM(density.shape, density.dtype)],
        halos[0],
        stored=(first_kernel, second_kernel, first_bias.reshape(1, -1), second_bias.reshape(1, -1), density),
        scratch=[
            pltpu.SemaphoreType.DMA((5,)),
            *[VMEM(kernel.shape, kernel.dtype) for kernel in (first_kernel, second_kernel)],
            *[VMEM((1, outputs), jnp.float32)] * 2,
        ],
    )
    if sides() == 1:
        place = lax.axis_index("ch")
        inner = (place == 1) | (place == 2)
        handed = lax.ppermute(jnp.where(inner, last, own), "ch", [(0, 2), (3, 1), (1, 0), (2, 3)])
        others = [nearest, handed, last]
        pair, _ = lax.optimization_barrier((jnp.concatenate(halos, axis=0), last))
        halos = [pair, lax.ppermute(pair, "ch", pairings[2])]
    hidden = layer(
        [own, *others], halos, 2, rows + sides(), first_taps, first_bias, hidden_kernel, VMEM, True
    )
    blocks = [hidden, *channel_swaps(hidden)]
    out = layer(blocks, [], 0, rows, second_taps, second_bias, finish_kernel, jax.ShapeDtypeStruct, False)
    return out[None]


def solution(mesh):
    placed = (
        P("gx", "gy", "ch", None),
        P(None, None, None, "ch", None),
        P("ch"),
        P(None, None, None, "ch", None),
        P("ch"),
    )
    return jax.shard_map(
        per_device, mesh=mesh, in_specs=placed, out_specs=P("gx", "gy", "ch", None), check_vma=False
    )
```

```python
import functools

import jax
import jax.numpy as jnp
from jax import lax
from jax.experimental import pallas as pl
from jax.experimental.pallas import tpu as pltpu
from jax.sharding import PartitionSpec as P

VMEM_BYTES = 12 << 20
VMEM = pltpu.VMEM
SENT = (2, 1)
IDLE = (True, False)
NEAR_FIRST = (True, False)


def call(kernel, name, out_shape, *operands, stored=(), scratch=(), flops=0):
    spec = pl.BlockSpec(memory_space=VMEM)
    return pl.pallas_call(
        kernel,
        out_shape=out_shape,
        in_specs=[pl.BlockSpec(memory_space=pltpu.HBM)] * len(stored) + [spec] * len(operands),
        out_specs=[spec] * len(out_shape),
        scratch_shapes=scratch,
        compiler_params=pltpu.CompilerParams(vmem_limit_bytes=VMEM_BYTES),
        cost_estimate=pl.CostEstimate(flops=flops, bytes_accessed=0, transcendentals=0),
        name=name,
    )(
        *[pltpu.with_memory_space_constraint(operand, pltpu.HBM) for operand in stored],
        *[pltpu.with_memory_space_constraint(operand, VMEM) for operand in operands],
    )


def sides():
    return 1 if lax.axis_size("gy") == 2 else 2


def partners():
    count = lax.axis_size("ch")
    return [[(i, i ^ step) for i in range(count)] for step in range(count)]


def channel_swaps(block):
    return [lax.ppermute(block, "ch", pairs) for pairs in partners()[1:]]


def edge_moves(edge, step, pairings):
    rows, channels = lax.axis_size("gy"), lax.axis_size("ch")
    if rows == 2:
        along = [(0, 1), (1, 0)]
    else:
        along = [(i, i + step) for i in range(rows) if 0 <= i + step < rows]
    return [
        lax.ppermute(edge, ("gy", "ch"), [(i * channels + c, j * channels + d) for i, j in along for c, d in pairs])
        for pairs in pairings
    ]


def far_pairs(idle):
    planes, rows = lax.axis_size("gx"), lax.axis_size("gy")
    pairs = [(i, i + 1, g, g) for i in range(1, planes - 1, 2) for g in range(rows)]
    if idle:
        alone = [(i * rows + g, i * rows + g) for i in (0, planes - 1) for g in range(rows)]
    else:
        alone = []
        pairs += [(i, i, g, g + 1) for i in (0, planes - 1) for g in range(0, rows, 2)]
    there = [(i * rows + g, j * rows + h) for i, j, g, h in pairs]
    return alone + there + [(j, i) for i, j in there]


def prepare_kernel(*refs):
    stored = refs[:5]
    first_taps, second_taps, first_bias, second_bias, own, copies, first_ref, second_ref, *bias_refs = refs[-10:]
    moves = [
        pltpu.make_async_copy(source, target, copies.at[i])
        for i, (source, target) in enumerate(zip(stored, (first_ref, second_ref, *bias_refs, own)))
    ]
    for move in moves:
        move.start()
    for move in moves:
        move.wait()
    gx = lax.axis_index("gx")
    outputs, inputs = first_ref.shape[3:]
    far = jnp.where(gx % 2 == 0, 2, 0)
    outer = jnp.full((outputs, inputs), (gx == 0) | (gx == lax.axis_size("gx") - 1))
    for kernel_ref, out in ((first_ref, first_taps), (second_ref, second_taps)):
        for slot, a in enumerate((far, 2 - far, 1)):
            for b in range(3):
                for c in range(3):
                    tap = kernel_ref[a, b, c]
                    if slot == 0:
                        tap = jnp.where(outer, 0.0, tap)
                    first = (slot * 3 + c) * outputs
                    out[first : first + outputs, b * inputs : (b + 1) * inputs] = tap
    at = [lax.broadcasted_iota(jnp.int32, (outputs, outputs), axis) for axis in range(2)]
    for bias_ref, out in zip(bias_refs, (first_bias, second_bias)):
        column = jnp.sum(jnp.where(at[0] == at[1], bias_ref[...], 0.0), axis=1, keepdims=True)
        out[...] = jnp.broadcast_to(column, out.shape)


def terms(taps, volume, slots, outs):
    rows, outputs, depth = outs[0].shape
    inputs = volume.shape[1]
    lane = lax.broadcasted_iota(jnp.int32, (outputs, depth), 1)
    for y in [*range(0, rows - 1, 2)] + [rows - 2] * (rows % 2):
        window = jnp.concatenate(
            [volume[y + i : y + i + 3].reshape(3 * inputs, depth) for i in range(2)], axis=1
        )
        product = jnp.dot(taps, window, preferred_element_type=jnp.float32)
        for i in range(2):
            for slot, out in zip(slots, outs):
                first, middle, last = (
                    product[(slot * 3 + c) * outputs : (slot * 3 + c + 1) * outputs, i * depth : (i + 1) * depth]
                    for c in range(3)
                )
                total = (
                    middle
                    + jnp.where(lane == 0, 0.0, pltpu.roll(first, 1, 1))
                    + jnp.where(lane == depth - 1, 0.0, pltpu.roll(last, depth - 1, 1))
                )
                out[y + i] = total.astype(out.dtype)


def beside_kernel(count, halo, steps, sent, taps_ref, *refs):
    blocks, refs = refs[:count], refs[count:]
    outs, volume = refs[-1 - sent : -1], refs[-1]
    halos = refs[: -1 - sent]
    rows, part, depth = blocks[0].shape
    place, low = lax.axis_index("ch"), lax.axis_index("gy") == 0
    if sides() == 1:
        own, beside = jnp.where(low, 1, halo), jnp.where(low, 1 + rows, 0)
        outside = jnp.where(low, 0, volume.shape[0] - 1)
        volume[outside] = jnp.zeros((part * count, depth), volume.dtype)
    else:
        own = halo
    def channels(step):
        source = jnp.bitwise_xor(place, step % count)
        return pl.ds(pl.multiple_of(source * part, part), part)

    for step, block in zip(steps, blocks):
        volume[pl.ds(own, rows), channels(step), :] = block[...]
    step = 0
    for ref in halos:
        for first in range(0, ref.shape[0], halo):
            if sides() == 1:
                at = beside
            else:
                at = 0 if step < count else halo + rows
            volume[pl.ds(at, halo), channels(step), :] = ref[first : first + halo]
            step += 1
    terms(taps_ref[: 3 * sent * outs[0].shape[1]], volume, range(sent), outs)


def center_kernel(taps_ref, volume, *outs):
    terms(taps_ref[3 * (3 - len(outs)) * outs[0].shape[1] :], volume, range(len(outs)), outs)


def finish_kernel(near_ref, center_ref, far_ref, bias_ref, out_ref):
    total = center_ref[...] + near_ref[...].astype(jnp.float32) + far_ref[...].astype(jnp.float32)
    out_ref[...] = jnp.maximum(total + bias_ref[...][None], 0.0).astype(out_ref.dtype)


def hidden_kernel(near_ref, center_ref, far_ref, bias_ref, out_ref):
    finish_kernel(near_ref, center_ref, far_ref, bias_ref, out_ref)
    if lax.axis_size("gy") > 2:
        gy, rows = lax.axis_index("gy"), out_ref.shape[0]
        for row, outside in ((0, gy == 0), (rows - 1, gy == lax.axis_size("gy") - 1)):
            kept = out_ref[row]
            out_ref[row] = jnp.where(jnp.full(kept.shape, outside), 0.0, kept)


def layer(blocks, steps, halos, halo, rows, taps, bias, kernel, out_type, last):
    count = len(blocks)
    _, part, depth = blocks[0].shape
    outputs = taps.shape[0] // 9
    flops = 2 * rows * depth * taps.shape[0] * taps.shape[1]
    side = VMEM((rows, outputs, depth), jnp.bfloat16)
    side = VMEM((rows, outputs, depth), jnp.bfloat16)
    sent = SENT[last]
    *outs, volume = call(
        functools.partial(beside_kernel, count, halo, steps, sent),
        "beside",
        [side] * sent + [VMEM((rows + 2, part * count, depth), jnp.bfloat16)],
        taps,
        *blocks,
        *halos,
        flops=sent * flops // 3,
    )
    planes = lax.axis_size("gx")
    far = lax.ppermute(outs[0], ("gx", "gy"), far_pairs(IDLE[last]))
    outs += call(
        center_kernel,
        "center",
        [side] * (2 - sent) + [VMEM((rows, outputs, depth), jnp.float32)],
        taps,
        volume,
        flops=(3 - sent) * flops // 3,
    )
    center = outs[2]
    near = lax.ppermute(outs[1], "gx", [(i, i ^ 1) for i in range(planes)])
    both = (near, center, far) if NEAR_FIRST[last] else (far, center, near)
    (out,) = call(kernel, "finish", [out_type((rows, outputs, depth), jnp.bfloat16)], *both, bias)
    return out


def per_device(density, first_kernel, first_bias, second_kernel, second_bias):
    density = density[0]
    rows, part, depth = density.shape
    outputs = first_kernel.shape[3]
    count = lax.axis_size("ch")
    pairings = partners()
    if sides() == 1:
        start = jnp.where(lax.axis_index("gy") == 0, rows - 2, 0)
        halos = edge_moves(lax.dynamic_slice_in_dim(density, start, 2, 0), 1, pairings[:2])
        last = lax.ppermute(density, "ch", pairings[-1])
        nearest = lax.ppermute(density, "ch", pairings[1])
    else:
        halos = edge_moves(density[-2:], 1, pairings) + edge_moves(density[:2], -1, pairings)
        others = channel_swaps(density)
    taps_shape = VMEM((9 * outputs, 3 * part * count), jnp.bfloat16)
    bias_shape = VMEM((outputs, depth), jnp.float32)
    first_taps, second_taps, first_bias, second_bias, own = call(
        prepare_kernel,
        "prepare",
        [taps_shape, taps_shape, bias_shape, bias_shape, VMEM(density.shape, density.dtype)],
        halos[0],
        stored=(first_kernel, second_kernel, first_bias.reshape(1, -1), second_bias.reshape(1, -1), density),
        scratch=[
            pltpu.SemaphoreType.DMA((5,)),
            *[VMEM(kernel.shape, kernel.dtype) for kernel in (first_kernel, second_kernel)],
            *[VMEM((1, outputs), jnp.float32)] * 2,
        ],
    )
    if sides() == 1:
        place = lax.axis_index("ch")
        inner = (place == 1) | (place == 2)
        handed = lax.ppermute(jnp.where(inner, last, own), "ch", [(0, 2), (3, 1), (1, 0), (2, 3)])
        others = [nearest, handed, last]
        pair = jnp.concatenate(halos, axis=0)
        pair, _ = lax.optimization_barrier((pair, last))
        halos = [pair, lax.ppermute(pair, "ch", pairings[2])]
    hidden = layer(
        [own, *others], [*range(count)], halos, 2, rows + sides(), first_taps, first_bias, hidden_kernel, VMEM, 0
    )
    order = sorted(range(1, count), key=lambda step: (step != count - 1, step))
    blocks = [hidden] + [lax.ppermute(hidden, "ch", pairings[step]) for step in order]
    out = layer(blocks, [0, *order], [], 0, rows, second_taps, second_bias, finish_kernel, jax.ShapeDtypeStruct, 1)
    return out[None]


def solution(mesh):
    placed = (
        P("gx", "gy", "ch", None),
        P(None, None, None, "ch", None),
        P("ch"),
        P(None, None, None, "ch", None),
        P("ch"),
    )
    return jax.shard_map(
        per_device, mesh=mesh, in_specs=placed, out_specs=P("gx", "gy", "ch", None), check_vma=False
    )
```

```python
import functools

import jax
import jax.numpy as jnp
from jax import lax
from jax.experimental import pallas as pl
from jax.experimental.pallas import tpu as pltpu
from jax.sharding import PartitionSpec as P

VMEM_BYTES = 12 << 20
VMEM = pltpu.VMEM
SENT = (2, 1)
IDLE = (True, False)
NEAR_FIRST = (True, False)


def call(kernel, name, out_shape, *operands, stored=(), scratch=(), flops=0):
    spec = pl.BlockSpec(memory_space=VMEM)
    return pl.pallas_call(
        kernel,
        out_shape=out_shape,
        in_specs=[pl.BlockSpec(memory_space=pltpu.HBM)] * len(stored) + [spec] * len(operands),
        out_specs=[spec] * len(out_shape),
        scratch_shapes=scratch,
        compiler_params=pltpu.CompilerParams(vmem_limit_bytes=VMEM_BYTES),
        cost_estimate=pl.CostEstimate(flops=flops, bytes_accessed=0, transcendentals=0),
        name=name,
    )(
        *[pltpu.with_memory_space_constraint(operand, pltpu.HBM) for operand in stored],
        *[pltpu.with_memory_space_constraint(operand, VMEM) for operand in operands],
    )


def sides():
    return 1 if lax.axis_size("gy") == 2 else 2


def partners():
    count = lax.axis_size("ch")
    return [[(i, i ^ step) for i in range(count)] for step in range(count)]


def swapped(step):
    return lambda place: jnp.bitwise_xor(place, step)


def passed(step):
    count = lax.axis_size("ch")
    return lambda place: lax.rem(place + (count - step) % count, count)


def round_ch(block, step):
    count = lax.axis_size("ch")
    return lax.ppermute(block, "ch", [(i, (i + step) % count) for i in range(count)])


def edge_moves(edge, step, pairings):
    rows, channels = lax.axis_size("gy"), lax.axis_size("ch")
    if rows == 2:
        along = [(0, 1), (1, 0)]
    else:
        along = [(i, i + step) for i in range(rows) if 0 <= i + step < rows]
    return [
        lax.ppermute(edge, ("gy", "ch"), [(i * channels + c, j * channels + d) for i, j in along for c, d in pairs])
        for pairs in pairings
    ]


def far_pairs(idle):
    planes, rows = lax.axis_size("gx"), lax.axis_size("gy")
    pairs = [(i, i + 1, g, g) for i in range(1, planes - 1, 2) for g in range(rows)]
    if idle:
        alone = [(i * rows + g, i * rows + g) for i in (0, planes - 1) for g in range(rows)]
    else:
        alone = []
        pairs += [(i, i, g, g + 1) for i in (0, planes - 1) for g in range(0, rows, 2)]
    there = [(i * rows + g, j * rows + h) for i, j, g, h in pairs]
    return alone + there + [(j, i) for i, j in there]


def prepare_kernel(*refs):
    stored = refs[:5]
    first_taps, second_taps, first_bias, second_bias, own, copies, first_ref, second_ref, *bias_refs = refs[-10:]
    moves = [
        pltpu.make_async_copy(source, target, copies.at[i])
        for i, (source, target) in enumerate(zip(stored, (first_ref, second_ref, *bias_refs, own)))
    ]
    for move in moves:
        move.start()
    for move in moves:
        move.wait()
    gx = lax.axis_index("gx")
    outputs, inputs = first_ref.shape[3:]
    far = jnp.where(gx % 2 == 0, 2, 0)
    outer = jnp.full((outputs, inputs), (gx == 0) | (gx == lax.axis_size("gx") - 1))
    for kernel_ref, out in ((first_ref, first_taps), (second_ref, second_taps)):
        for slot, a in enumerate((far, 2 - far, 1)):
            for b in range(3):
                for c in range(3):
                    tap = kernel_ref[a, b, c]
                    if slot == 0:
                        tap = jnp.where(outer, 0.0, tap)
                    first = (slot * 3 + c) * outputs
                    out[first : first + outputs, b * inputs : (b + 1) * inputs] = tap
    at = [lax.broadcasted_iota(jnp.int32, (outputs, outputs), axis) for axis in range(2)]
    for bias_ref, out in zip(bias_refs, (first_bias, second_bias)):
        column = jnp.sum(jnp.where(at[0] == at[1], bias_ref[...], 0.0), axis=1, keepdims=True)
        out[...] = jnp.broadcast_to(column, out.shape)


def terms(taps, volume, slots, outs):
    rows, outputs, depth = outs[0].shape
    inputs = volume.shape[1]
    lane = lax.broadcasted_iota(jnp.int32, (outputs, depth), 1)
    for y in [*range(0, rows - 1, 2)] + [rows - 2] * (rows % 2):
        window = jnp.concatenate(
            [volume[y + i : y + i + 3].reshape(3 * inputs, depth) for i in range(2)], axis=1
        )
        product = jnp.dot(taps, window, preferred_element_type=jnp.float32)
        for i in range(2):
            for slot, out in zip(slots, outs):
                first, middle, last = (
                    product[(slot * 3 + c) * outputs : (slot * 3 + c + 1) * outputs, i * depth : (i + 1) * depth]
                    for c in range(3)
                )
                total = (
                    middle
                    + jnp.where(lane == 0, 0.0, pltpu.roll(first, 1, 1))
                    + jnp.where(lane == depth - 1, 0.0, pltpu.roll(last, depth - 1, 1))
                )
                out[y + i] = total.astype(out.dtype)


def beside_kernel(count, halo, sources, sent, taps_ref, *refs):
    blocks, refs = refs[:count], refs[count:]
    outs, volume = refs[-1 - sent : -1], refs[-1]
    halos = refs[: -1 - sent]
    rows, part, depth = blocks[0].shape
    place, low = lax.axis_index("ch"), lax.axis_index("gy") == 0
    if sides() == 1:
        own, beside = jnp.where(low, 1, halo), jnp.where(low, 1 + rows, 0)
        outside = jnp.where(low, 0, volume.shape[0] - 1)
        volume[outside] = jnp.zeros((part * count, depth), volume.dtype)
    else:
        own = halo
    def channels(source):
        return pl.ds(pl.multiple_of(source(place) * part, part), part)

    for source, block in zip(sources, blocks):
        volume[pl.ds(own, rows), channels(source), :] = block[...]
    edges = [ref.at[first : first + halo] for ref in halos for first in range(0, ref.shape[0], halo)]
    for step, edge in enumerate(edges):
        at = beside if sides() == 1 else 0 if step < count else halo + rows
        volume[pl.ds(at, halo), channels(swapped(step % count)), :] = edge[...]
    terms(taps_ref[: 3 * sent * outs[0].shape[1]], volume, range(sent), outs)


def center_kernel(taps_ref, volume, *outs):
    terms(taps_ref[3 * (3 - len(outs)) * outs[0].shape[1] :], volume, range(len(outs)), outs)


def finish_kernel(near_ref, center_ref, far_ref, bias_ref, out_ref):
    total = center_ref[...] + near_ref[...].astype(jnp.float32) + far_ref[...].astype(jnp.float32)
    out_ref[...] = jnp.maximum(total + bias_ref[...][None], 0.0).astype(out_ref.dtype)


def hidden_kernel(near_ref, center_ref, far_ref, bias_ref, out_ref):
    finish_kernel(near_ref, center_ref, far_ref, bias_ref, out_ref)
    if lax.axis_size("gy") > 2:
        gy, rows = lax.axis_index("gy"), out_ref.shape[0]
        for row, outside in ((0, gy == 0), (rows - 1, gy == lax.axis_size("gy") - 1)):
            kept = out_ref[row]
            out_ref[row] = jnp.where(jnp.full(kept.shape, outside), 0.0, kept)


def layer(blocks, sources, halos, halo, rows, taps, bias, kernel, out_type, last):
    count = len(blocks)
    _, part, depth = blocks[0].shape
    outputs = taps.shape[0] // 9
    flops = 2 * rows * depth * taps.shape[0] * taps.shape[1]
    side = VMEM((rows, outputs, depth), jnp.bfloat16)
    side = VMEM((rows, outputs, depth), jnp.bfloat16)
    sent = SENT[last]
    *outs, volume = call(
        functools.partial(beside_kernel, count, halo, sources, sent),
        "beside",
        [side] * sent + [VMEM((rows + 2, part * count, depth), jnp.bfloat16)],
        taps,
        *blocks,
        *halos,
        flops=sent * flops // 3,
    )
    planes = lax.axis_size("gx")
    far = lax.ppermute(outs[0], ("gx", "gy"), far_pairs(IDLE[last]))
    outs += call(
        center_kernel,
        "center",
        [side] * (2 - sent) + [VMEM((rows, outputs, depth), jnp.float32)],
        taps,
        volume,
        flops=(3 - sent) * flops // 3,
    )
    center = outs[2]
    near = lax.ppermute(outs[1], "gx", [(i, i ^ 1) for i in range(planes)])
    both = (near, center, far) if NEAR_FIRST[last] else (far, center, near)
    (out,) = call(kernel, "finish", [out_type((rows, outputs, depth), jnp.bfloat16)], *both, bias)
    return out


def per_device(density, first_kernel, first_bias, second_kernel, second_bias):
    density = density[0]
    rows, part, depth = density.shape
    outputs = first_kernel.shape[3]
    count = lax.axis_size("ch")
    pairings = partners()
    one_sided = sides() == 1
    if one_sided:
        start = jnp.where(lax.axis_index("gy") == 0, rows - 2, 0)
        halos = edge_moves(lax.dynamic_slice_in_dim(density, start, 2, 0), 1, pairings[:2])
        upward, downward = round_ch(density, 1), round_ch(density, -1)
    else:
        halos = edge_moves(density[-2:], 1, pairings) + edge_moves(density[:2], -1, pairings)
        others = [lax.ppermute(density, "ch", pairs) for pairs in pairings[1:]]
        sources = [swapped(step) for step in range(count)]
    taps_shape = VMEM((9 * outputs, 3 * part * count), jnp.bfloat16)
    bias_shape = VMEM((outputs, depth), jnp.float32)
    first_taps, second_taps, first_bias, second_bias, own = call(
        prepare_kernel,
        "prepare",
        [taps_shape, taps_shape, bias_shape, bias_shape, VMEM(density.shape, density.dtype)],
        halos[0],
        stored=(first_kernel, second_kernel, first_bias.reshape(1, -1), second_bias.reshape(1, -1), density),
        scratch=[
            pltpu.SemaphoreType.DMA((5,)),
            *[VMEM(kernel.shape, kernel.dtype) for kernel in (first_kernel, second_kernel)],
            *[VMEM((1, outputs), jnp.float32)] * 2,
        ],
    )
    if one_sided:
        others = [downward, round_ch(upward, 1), upward]
        sources = [passed(step) for step in (0, -1, 2, 1)]
        pair, _ = lax.optimization_barrier((jnp.concatenate(halos, axis=0), upward))
        halos = [pair, lax.ppermute(pair, "ch", pairings[2])]
    hidden = layer(
        [own, *others], sources, halos, 2, rows + sides(), first_taps, first_bias, hidden_kernel, VMEM, 0
    )
    order = sorted(range(1, count), key=lambda step: (step != count - 1, step))
    blocks = [hidden] + [lax.ppermute(hidden, "ch", pairings[step]) for step in order]
    sources = [swapped(step) for step in (0, *order)]
    out = layer(blocks, sources, [], 0, rows, second_taps, second_bias, finish_kernel, jax.ShapeDtypeStruct, 1)
    return out[None]


def solution(mesh):
    placed = (
        P("gx", "gy", "ch", None),
        P(None, None, None, "ch", None),
        P("ch"),
        P(None, None, None, "ch", None),
        P("ch"),
    )
    return jax.shard_map(
        per_device, mesh=mesh, in_specs=placed, out_specs=P("gx", "gy", "ch", None), check_vma=False
    )
```

```python
import functools

import jax
import jax.numpy as jnp
from jax import lax
from jax.experimental import pallas as pl
from jax.experimental.pallas import tpu as pltpu
from jax.sharding import PartitionSpec as P

VMEM_BYTES = 12 << 20
VMEM = pltpu.VMEM
SENT = (2, 1)
IDLE = (True, False)
NEAR_FIRST = (True, False)


def call(kernel, name, out_shape, *operands, stored=(), scratch=(), flops=0):
    spec = pl.BlockSpec(memory_space=VMEM)
    return pl.pallas_call(
        kernel,
        out_shape=out_shape,
        in_specs=[pl.BlockSpec(memory_space=pltpu.HBM)] * len(stored) + [spec] * len(operands),
        out_specs=[spec] * len(out_shape),
        scratch_shapes=scratch,
        compiler_params=pltpu.CompilerParams(vmem_limit_bytes=VMEM_BYTES),
        cost_estimate=pl.CostEstimate(flops=flops, bytes_accessed=0, transcendentals=0),
        name=name,
    )(
        *[pltpu.with_memory_space_constraint(operand, pltpu.HBM) for operand in stored],
        *[pltpu.with_memory_space_constraint(operand, VMEM) for operand in operands],
    )


def sides():
    return 1 if lax.axis_size("gy") == 2 else 2


def partners():
    count = lax.axis_size("ch")
    return [[(i, i ^ step) for i in range(count)] for step in range(count)]


def swapped(step):
    return lambda place: jnp.bitwise_xor(place, step)


def passed(step):
    count = lax.axis_size("ch")
    return lambda place: lax.rem(place + (count - step) % count, count)


def round_ch(block, step):
    count = lax.axis_size("ch")
    return lax.ppermute(block, "ch", [(i, (i + step) % count) for i in range(count)])


def edge_moves(edge, step, pairings):
    rows, channels = lax.axis_size("gy"), lax.axis_size("ch")
    if rows == 2:
        along = [(0, 1), (1, 0)]
    else:
        along = [(i, i + step) for i in range(rows) if 0 <= i + step < rows]
    return [
        lax.ppermute(edge, ("gy", "ch"), [(i * channels + c, j * channels + d) for i, j in along for c, d in pairs])
        for pairs in pairings
    ]


def far_pairs(idle):
    planes, rows = lax.axis_size("gx"), lax.axis_size("gy")
    pairs = [(i, i + 1, g, g) for i in range(1, planes - 1, 2) for g in range(rows)]
    if idle:
        alone = [(i * rows + g, i * rows + g) for i in (0, planes - 1) for g in range(rows)]
    else:
        alone = []
        pairs += [(i, i, g, g + 1) for i in (0, planes - 1) for g in range(0, rows, 2)]
    there = [(i * rows + g, j * rows + h) for i, j, g, h in pairs]
    return alone + there + [(j, i) for i, j in there]


def edge_kernel(density_ref, edge_ref, copied):
    first = jnp.where(lax.axis_index("gy") == 0, density_ref.shape[0] - 2, 0)
    move = pltpu.make_async_copy(density_ref.at[pl.ds(first, 2)], edge_ref, copied)
    move.start()
    move.wait()


def prepare_kernel(*refs):
    stored = refs[:5]
    first_taps, second_taps, first_bias, second_bias, own, copies, first_ref, second_ref, *bias_refs = refs[-10:]
    moves = [
        pltpu.make_async_copy(source, target, copies.at[i])
        for i, (source, target) in enumerate(zip(stored, (first_ref, second_ref, *bias_refs, own)))
    ]
    for move in moves:
        move.start()
    for move in moves:
        move.wait()
    gx = lax.axis_index("gx")
    outputs, inputs = first_ref.shape[3:]
    far = jnp.where(gx % 2 == 0, 2, 0)
    outer = jnp.full((outputs, inputs), (gx == 0) | (gx == lax.axis_size("gx") - 1))
    for kernel_ref, out in ((first_ref, first_taps), (second_ref, second_taps)):
        for slot, a in enumerate((far, 2 - far, 1)):
            for b in range(3):
                for c in range(3):
                    tap = kernel_ref[a, b, c]
                    if slot == 0:
                        tap = jnp.where(outer, 0.0, tap)
                    first = (slot * 3 + c) * outputs
                    out[first : first + outputs, b * inputs : (b + 1) * inputs] = tap
    at = [lax.broadcasted_iota(jnp.int32, (outputs, outputs), axis) for axis in range(2)]
    for bias_ref, out in zip(bias_refs, (first_bias, second_bias)):
        column = jnp.sum(jnp.where(at[0] == at[1], bias_ref[...], 0.0), axis=1, keepdims=True)
        out[...] = jnp.broadcast_to(column, out.shape)


def terms(taps, volume, slots, outs):
    rows, outputs, depth = outs[0].shape
    inputs = volume.shape[1]
    lane = lax.broadcasted_iota(jnp.int32, (outputs, depth), 1)
    for y in [*range(0, rows - 1, 2)] + [rows - 2] * (rows % 2):
        window = jnp.concatenate(
            [volume[y + i : y + i + 3].reshape(3 * inputs, depth) for i in range(2)], axis=1
        )
        product = jnp.dot(taps, window, preferred_element_type=jnp.float32)
        for i in range(2):
            for slot, out in zip(slots, outs):
                first, middle, last = (
                    product[(slot * 3 + c) * outputs : (slot * 3 + c + 1) * outputs, i * depth : (i + 1) * depth]
                    for c in range(3)
                )
                total = (
                    middle
                    + jnp.where(lane == 0, 0.0, pltpu.roll(first, 1, 1))
                    + jnp.where(lane == depth - 1, 0.0, pltpu.roll(last, depth - 1, 1))
                )
                out[y + i] = total.astype(out.dtype)


def beside_kernel(count, halo, sources, sent, taps_ref, *refs):
    blocks, refs = refs[:count], refs[count:]
    outs, volume = refs[-1 - sent : -1], refs[-1]
    halos = refs[: -1 - sent]
    rows, part, depth = blocks[0].shape
    place, low = lax.axis_index("ch"), lax.axis_index("gy") == 0
    if sides() == 1:
        own, beside = jnp.where(low, 1, halo), jnp.where(low, 1 + rows, 0)
        outside = jnp.where(low, 0, volume.shape[0] - 1)
        volume[outside] = jnp.zeros((part * count, depth), volume.dtype)
    else:
        own = halo
    def channels(source):
        return pl.ds(pl.multiple_of(source(place) * part, part), part)

    for source, block in zip(sources, blocks):
        volume[pl.ds(own, rows), channels(source), :] = block[...]
    edges = [ref.at[first : first + halo] for ref in halos for first in range(0, ref.shape[0], halo)]
    for step, edge in enumerate(edges):
        at = beside if sides() == 1 else 0 if step < count else halo + rows
        volume[pl.ds(at, halo), channels(swapped((0, 2, 1, 3)[step % count] if sides() == 1 else step % count)), :] = edge[...]
    terms(taps_ref[: 3 * sent * outs[0].shape[1]], volume, range(sent), outs)


def center_kernel(taps_ref, volume, *outs):
    terms(taps_ref[3 * (3 - len(outs)) * outs[0].shape[1] :], volume, range(len(outs)), outs)


def finish_kernel(near_ref, center_ref, far_ref, bias_ref, out_ref):
    total = center_ref[...] + near_ref[...].astype(jnp.float32) + far_ref[...].astype(jnp.float32)
    out_ref[...] = jnp.maximum(total + bias_ref[...][None], 0.0).astype(out_ref.dtype)


def hidden_kernel(near_ref, center_ref, far_ref, bias_ref, out_ref):
    finish_kernel(near_ref, center_ref, far_ref, bias_ref, out_ref)
    if lax.axis_size("gy") > 2:
        gy, rows = lax.axis_index("gy"), out_ref.shape[0]
        for row, outside in ((0, gy == 0), (rows - 1, gy == lax.axis_size("gy") - 1)):
            kept = out_ref[row]
            out_ref[row] = jnp.where(jnp.full(kept.shape, outside), 0.0, kept)


def layer(blocks, sources, halos, halo, rows, taps, bias, kernel, out_type, last):
    count = len(blocks)
    _, part, depth = blocks[0].shape
    outputs = taps.shape[0] // 9
    flops = 2 * rows * depth * taps.shape[0] * taps.shape[1]
    side = VMEM((rows, outputs, depth), jnp.bfloat16)
    side = VMEM((rows, outputs, depth), jnp.bfloat16)
    sent = SENT[last]
    *outs, volume = call(
        functools.partial(beside_kernel, count, halo, sources, sent),
        "beside",
        [side] * sent + [VMEM((rows + 2, part * count, depth), jnp.bfloat16)],
        taps,
        *blocks,
        *halos,
        flops=sent * flops // 3,
    )
    planes = lax.axis_size("gx")
    far = lax.ppermute(outs[0], ("gx", "gy"), far_pairs(IDLE[last]))
    outs += call(
        center_kernel,
        "center",
        [side] * (2 - sent) + [VMEM((rows, outputs, depth), jnp.float32)],
        taps,
        volume,
        flops=(3 - sent) * flops // 3,
    )
    center = outs[2]
    near = lax.ppermute(outs[1], "gx", [(i, i ^ 1) for i in range(planes)])
    both = (near, center, far) if NEAR_FIRST[last] else (far, center, near)
    (out,) = call(kernel, "finish", [out_type((rows, outputs, depth), jnp.bfloat16)], *both, bias)
    return out


def per_device(density, first_kernel, first_bias, second_kernel, second_bias):
    density = density[0]
    rows, part, depth = density.shape
    outputs = first_kernel.shape[3]
    count = lax.axis_size("ch")
    pairings = partners()
    one_sided = sides() == 1
    if one_sided:
        edge_shape = [VMEM((2, part, depth), density.dtype)]
        (edge,) = call(edge_kernel, "edge", edge_shape, stored=(density,), scratch=[pltpu.SemaphoreType.DMA])
        halos = edge_moves(edge, 1, [pairings[0], pairings[2]])
        upward, downward = round_ch(density, 1), round_ch(density, -1)
    else:
        halos = edge_moves(density[-2:], 1, pairings) + edge_moves(density[:2], -1, pairings)
        others = [lax.ppermute(density, "ch", pairs) for pairs in pairings[1:]]
        sources = [swapped(step) for step in range(count)]
    taps_shape = VMEM((9 * outputs, 3 * part * count), jnp.bfloat16)
    bias_shape = VMEM((outputs, depth), jnp.float32)
    first_taps, second_taps, first_bias, second_bias, own = call(
        prepare_kernel,
        "prepare",
        [taps_shape, taps_shape, bias_shape, bias_shape, VMEM(density.shape, density.dtype)],
        halos[0],
        stored=(first_kernel, second_kernel, first_bias.reshape(1, -1), second_bias.reshape(1, -1), density),
        scratch=[
            pltpu.SemaphoreType.DMA((5,)),
            *[VMEM(kernel.shape, kernel.dtype) for kernel in (first_kernel, second_kernel)],
            *[VMEM((1, outputs), jnp.float32)] * 2,
        ],
    )
    if one_sided:
        others = [downward, round_ch(upward, 1), upward]
        sources = [passed(step) for step in (0, -1, 2, 1)]
        pair, _ = lax.optimization_barrier((jnp.concatenate(halos, axis=0), upward))
        halos = [pair, lax.ppermute(pair, "ch", pairings[1])]
    hidden = layer(
        [own, *others], sources, halos, 2, rows + sides(), first_taps, first_bias, hidden_kernel, VMEM, 0
    )
    order = sorted(range(1, count), key=lambda step: (step != count - 1, step))
    blocks = [hidden] + [lax.ppermute(hidden, "ch", pairings[step]) for step in order]
    sources = [swapped(step) for step in (0, *order)]
    out = layer(blocks, sources, [], 0, rows, second_taps, second_bias, finish_kernel, jax.ShapeDtypeStruct, 1)
    return out[None]


def solution(mesh):
    placed = (
        P("gx", "gy", "ch", None),
        P(None, None, None, "ch", None),
        P("ch"),
        P(None, None, None, "ch", None),
        P("ch"),
    )
    return jax.shard_map(
        per_device, mesh=mesh, in_specs=placed, out_specs=P("gx", "gy", "ch", None), check_vma=False
    )
```

```python
import functools

import jax
import jax.numpy as jnp
from jax import lax
from jax.experimental import pallas as pl
from jax.experimental.pallas import tpu as pltpu
from jax.sharding import PartitionSpec as P

VMEM_BYTES = 12 << 20
VMEM = pltpu.VMEM
SENT = (2, 1)
IDLE = (True, False)
NEAR_FIRST = (True, False)


def call(kernel, name, out_shape, *operands, stored=(), scratch=(), flops=0):
    spec = pl.BlockSpec(memory_space=VMEM)
    return pl.pallas_call(
        kernel,
        out_shape=out_shape,
        in_specs=[pl.BlockSpec(memory_space=pltpu.HBM)] * len(stored) + [spec] * len(operands),
        out_specs=[spec] * len(out_shape),
        scratch_shapes=scratch,
        compiler_params=pltpu.CompilerParams(vmem_limit_bytes=VMEM_BYTES),
        cost_estimate=pl.CostEstimate(flops=flops, bytes_accessed=0, transcendentals=0),
        name=name,
    )(
        *[pltpu.with_memory_space_constraint(operand, pltpu.HBM) for operand in stored],
        *[pltpu.with_memory_space_constraint(operand, VMEM) for operand in operands],
    )


def sides():
    return 1 if lax.axis_size("gy") == 2 else 2


def partners():
    count = lax.axis_size("ch")
    return [[(i, i ^ step) for i in range(count)] for step in range(count)]


def swapped(step):
    return lambda place: jnp.bitwise_xor(place, step)


def passed(step):
    count = lax.axis_size("ch")
    return lambda place: lax.rem(place + (count - step) % count, count)


def round_ch(block, step):
    count = lax.axis_size("ch")
    return lax.ppermute(block, "ch", [(i, (i + step) % count) for i in range(count)])


def edge_moves(edge, step, pairings):
    rows, channels = lax.axis_size("gy"), lax.axis_size("ch")
    if rows == 2:
        along = [(0, 1), (1, 0)]
    else:
        along = [(i, i + step) for i in range(rows) if 0 <= i + step < rows]
    return [
        lax.ppermute(edge, ("gy", "ch"), [(i * channels + c, j * channels + d) for i, j in along for c, d in pairs])
        for pairs in pairings
    ]


def far_pairs(idle):
    planes, rows = lax.axis_size("gx"), lax.axis_size("gy")
    pairs = [(i, i + 1, g, g) for i in range(1, planes - 1, 2) for g in range(rows)]
    if idle:
        alone = [(i * rows + g, i * rows + g) for i in (0, planes - 1) for g in range(rows)]
    else:
        alone = []
        pairs += [(i, i, g, g + 1) for i in (0, planes - 1) for g in range(0, rows, 2)]
    there = [(i * rows + g, j * rows + h) for i, j, g, h in pairs]
    return alone + there + [(j, i) for i, j in there]


def edge_kernel(density_ref, edge_ref, copied):
    first = jnp.where(lax.axis_index("gy") == 0, density_ref.shape[0] - 2, 0)
    move = pltpu.make_async_copy(density_ref.at[pl.ds(first, 2)], edge_ref, copied)
    move.start()
    move.wait()


def prepare_kernel(*refs):
    stored = refs[:5]
    first_taps, second_taps, first_bias, second_bias, own, copies, first_ref, second_ref, *bias_refs = refs[-10:]
    moves = [
        pltpu.make_async_copy(source, target, copies.at[i])
        for i, (source, target) in enumerate(zip(stored, (first_ref, second_ref, *bias_refs, own)))
    ]
    for move in moves:
        move.start()
    for move in moves:
        move.wait()
    gx = lax.axis_index("gx")
    outputs, inputs = first_ref.shape[3:]
    far = jnp.where(gx % 2 == 0, 2, 0)
    outer = jnp.full((outputs, inputs), (gx == 0) | (gx == lax.axis_size("gx") - 1))
    for kernel_ref, out in ((first_ref, first_taps), (second_ref, second_taps)):
        for slot, a in enumerate((far, 2 - far, 1)):
            for b in range(3):
                for c in range(3):
                    tap = kernel_ref[a, b, c]
                    if slot == 0:
                        tap = jnp.where(outer, 0.0, tap)
                    first = (slot * 3 + c) * outputs
                    out[first : first + outputs, b * inputs : (b + 1) * inputs] = tap
    at = [lax.broadcasted_iota(jnp.int32, (outputs, outputs), axis) for axis in range(2)]
    for bias_ref, out in zip(bias_refs, (first_bias, second_bias)):
        column = jnp.sum(jnp.where(at[0] == at[1], bias_ref[...], 0.0), axis=1, keepdims=True)
        out[...] = jnp.broadcast_to(column, out.shape)


def terms(taps, volume, slots, outs):
    rows, outputs, depth = outs[0].shape
    inputs = volume.shape[1]
    lane = lax.broadcasted_iota(jnp.int32, (outputs, depth), 1)
    for y in [*range(0, rows - 1, 2)] + [rows - 2] * (rows % 2):
        window = jnp.concatenate(
            [volume[y + i : y + i + 3].reshape(3 * inputs, depth) for i in range(2)], axis=1
        )
        product = jnp.dot(taps, window, preferred_element_type=jnp.float32)
        for i in range(2):
            for slot, out in zip(slots, outs):
                first, middle, last = (
                    product[(slot * 3 + c) * outputs : (slot * 3 + c + 1) * outputs, i * depth : (i + 1) * depth]
                    for c in range(3)
                )
                total = (
                    middle
                    + jnp.where(lane == 0, 0.0, pltpu.roll(first, 1, 1))
                    + jnp.where(lane == depth - 1, 0.0, pltpu.roll(last, depth - 1, 1))
                )
                out[y + i] = total.astype(out.dtype)


def beside_kernel(count, halo, sources, sent, taps_ref, *refs):
    blocks, refs = refs[:count], refs[count:]
    outs, volume = refs[-1 - sent : -1], refs[-1]
    halos = refs[: -1 - sent]
    rows, part, depth = blocks[0].shape
    place, low = lax.axis_index("ch"), lax.axis_index("gy") == 0
    if sides() == 1:
        own, beside = jnp.where(low, 1, halo), jnp.where(low, 1 + rows, 0)
        outside = jnp.where(low, 0, volume.shape[0] - 1)
        volume[outside] = jnp.zeros((part * count, depth), volume.dtype)
    else:
        own = halo
    def channels(source):
        return pl.ds(pl.multiple_of(source(place) * part, part), part)

    for source, block in zip(sources, blocks):
        volume[pl.ds(own, rows), channels(source), :] = block[...]
    edges = [ref.at[first : first + halo] for ref in halos for first in range(0, ref.shape[0], halo)]
    for step, edge in enumerate(edges):
        at = beside if sides() == 1 else 0 if step < count else halo + rows
        volume[pl.ds(at, halo), channels(swapped((0, 2, 1, 3)[step % count] if sides() == 1 else step % count)), :] = edge[...]
    terms(taps_ref[: 3 * sent * outs[0].shape[1]], volume, range(sent), outs)


def center_kernel(taps_ref, volume, *outs):
    terms(taps_ref[3 * (3 - len(outs)) * outs[0].shape[1] :], volume, range(len(outs)), outs)


def finish_kernel(near_ref, center_ref, far_ref, bias_ref, out_ref):
    total = center_ref[...] + near_ref[...].astype(jnp.float32) + far_ref[...].astype(jnp.float32)
    out_ref[...] = jnp.maximum(total + bias_ref[...][None], 0.0).astype(out_ref.dtype)


def hidden_kernel(near_ref, center_ref, far_ref, bias_ref, out_ref):
    finish_kernel(near_ref, center_ref, far_ref, bias_ref, out_ref)
    if lax.axis_size("gy") > 2:
        gy, rows = lax.axis_index("gy"), out_ref.shape[0]
        for row, outside in ((0, gy == 0), (rows - 1, gy == lax.axis_size("gy") - 1)):
            kept = out_ref[row]
            out_ref[row] = jnp.where(jnp.full(kept.shape, outside), 0.0, kept)


def layer(blocks, sources, halos, halo, rows, taps, bias, kernel, out_type, last):
    count = len(blocks)
    _, part, depth = blocks[0].shape
    outputs = taps.shape[0] // 9
    flops = 2 * rows * depth * taps.shape[0] * taps.shape[1]
    side = VMEM((rows, outputs, depth), jnp.bfloat16)
    side = VMEM((rows, outputs, depth), jnp.bfloat16)
    sent = SENT[last]
    *outs, volume = call(
        functools.partial(beside_kernel, count, halo, sources, sent),
        "beside",
        [side] * sent + [VMEM((rows + 2, part * count, depth), jnp.bfloat16)],
        taps,
        *blocks,
        *halos,
        flops=sent * flops // 3,
    )
    planes = lax.axis_size("gx")
    far = lax.ppermute(outs[0], ("gx", "gy"), far_pairs(IDLE[last]))
    outs += call(
        center_kernel,
        "center",
        [side] * (2 - sent) + [VMEM((rows, outputs, depth), jnp.float32)],
        taps,
        volume,
        flops=(3 - sent) * flops // 3,
    )
    center = outs[2]
    near = lax.ppermute(outs[1], "gx", [(i, i ^ 1) for i in range(planes)])
    both = (near, center, far) if NEAR_FIRST[last] else (far, center, near)
    (out,) = call(kernel, "finish", [out_type((rows, outputs, depth), jnp.bfloat16)], *both, bias)
    return out


def per_device(density, first_kernel, first_bias, second_kernel, second_bias):
    density = density[0]
    rows, part, depth = density.shape
    outputs = first_kernel.shape[3]
    count = lax.axis_size("ch")
    pairings = partners()
    one_sided = sides() == 1
    if one_sided:
        edge_shape = [VMEM((2, part, depth), density.dtype)]
        (edge,) = call(edge_kernel, "edge", edge_shape, stored=(density,), scratch=[pltpu.SemaphoreType.DMA])
        halos = edge_moves(edge, 1, [pairings[0], pairings[2]])
        upward, downward = round_ch(density, 1), round_ch(density, -1)
    else:
        halos = edge_moves(density[-2:], 1, pairings) + edge_moves(density[:2], -1, pairings)
        others = [lax.ppermute(density, "ch", pairs) for pairs in pairings[1:]]
        sources = [swapped(step) for step in range(count)]
    taps_shape = VMEM((9 * outputs, 3 * part * count), jnp.bfloat16)
    bias_shape = VMEM((outputs, depth), jnp.float32)
    first_taps, second_taps, first_bias, second_bias, own = call(
        prepare_kernel,
        "prepare",
        [taps_shape, taps_shape, bias_shape, bias_shape, VMEM(density.shape, density.dtype)],
        halos[1],
        stored=(first_kernel, second_kernel, first_bias.reshape(1, -1), second_bias.reshape(1, -1), density),
        scratch=[
            pltpu.SemaphoreType.DMA((5,)),
            *[VMEM(kernel.shape, kernel.dtype) for kernel in (first_kernel, second_kernel)],
            *[VMEM((1, outputs), jnp.float32)] * 2,
        ],
    )
    if one_sided:
        others = [downward, round_ch(upward, 1), upward]
        sources = [passed(step) for step in (0, -1, 2, 1)]
        pair, _ = lax.optimization_barrier((jnp.concatenate(halos, axis=0), upward))
        halos = [pair, lax.ppermute(pair, "ch", pairings[1])]
    hidden = layer(
        [own, *others], sources, halos, 2, rows + sides(), first_taps, first_bias, hidden_kernel, VMEM, 0
    )
    order = sorted(range(1, count), key=lambda step: (step != count - 1, step))
    blocks = [hidden] + [lax.ppermute(hidden, "ch", pairings[step]) for step in order]
    sources = [swapped(step) for step in (0, *order)]
    out = layer(blocks, sources, [], 0, rows, second_taps, second_bias, finish_kernel, jax.ShapeDtypeStruct, 1)
    return out[None]


def solution(mesh):
    placed = (
        P("gx", "gy", "ch", None),
        P(None, None, None, "ch", None),
        P("ch"),
        P(None, None, None, "ch", None),
        P("ch"),
    )
    return jax.shard_map(
        per_device, mesh=mesh, in_specs=placed, out_specs=P("gx", "gy", "ch", None), check_vma=False
    )
```
